32 devices in a mesh: groups: 2 (over x), seq: 4 (over y, core), fsdp: 4 (over z).
Axes of the slice: x: 2, y: 2, z: 4, core: 2. Of those that a mesh axis runs over, the one named last changes fastest.
Arguments:
- tokens: bfloat16 [12288, 1536], P(('groups', 'seq', 'fsdp')), parts along dimension 0, may hold values from -6 to 6
- mod_shift: float32 [3072], P('groups'), parts along dimension 0, may hold values from -3 to 3
- mod_scale: float32 [3072], P('groups'), parts along dimension 0, may hold values from -2.5 to 2.5
- qkv_weight: bfloat16 [1536, 4608], P(('seq', 'fsdp')), may hold values from -0.15625 to 0.15625
- gain_q: float32 [1536], replicated, may hold values from 0.1 to 1.9
- gain_k: float32 [1536], replicated, may hold values from 0.1 to 1.9
- stale_kv: bfloat16 [12288, 3072], P(('groups', 'seq', 'fsdp')), parts along dimension 0, may hold values from -110 to 110
- tile_place: int32 [32], P('groups'), parts along dimension 0, may hold values from 0 to 15, as said below
- reader_lists: int32 [32, 2], P(('groups', 'seq', 'fsdp')), parts along dimension 0, may hold values from 0 to 15, as said below
- window_masks: int32 [32, 2, 3], P(('groups', 'seq', 'fsdp')), parts along dimension 0, may hold values 0 or 1
Outputs:
- attended: bfloat16 [12288, 1536], P(('groups', 'seq', 'fsdp')), parts along dimension 0
The draws below stay inside these ranges and needn't reach their ends.
There are 2 independent parts, one for each index of `groups`. The reference program is written for one: setup_inputs(seed, part) draws one part's arguments, and reference() takes and returns one part's arrays. A program takes and returns all parts, laid end to end along the dimension named above; an argument that names none is the same for every part. Nothing has to cross between parts.
Inputs may be any that keep to these rules, and one draw needn't show every extreme that they name: `tile_place`: a permutation of the tiles. `reader_lists`: each row r names 2 different tiles, each placed in a row block of a device other than r // 1 and at most 2 devices away from it.
All inputs are finite; a program needn't handle non-finite values. No bound on the sum of `window_masks` on one device may be relied on, other than what follows from the above.
Results may differ from the reference program's by a relative error of at most 0.003.
The reference program's roundings to bfloat16 on the way count: a program that leaves them out, or rounds other values in their place, can miss the bound.
Values may be sent and summed in bfloat16 or wider, within the bound.
No kernel may reach another device: no remote copies, remote signals or barrier semaphores. Data moves between devices by JAX's collectives and lax.ppermute only.
A program may use at most 128 MiB of HBM per device.

```python
import jax
import jax.numpy as jnp
from jax import lax

D = 1536
HEAD = 128
HEADS = 12
TILE = 384
KBLK = 128
NEED = 2
REACH = 2
TILE_DEV = 1
HW = 1536
KB = 3
TILES = 16
TOKENS = 6144


def tile_order(key):
    return jax.random.permutation(jax.random.fold_in(key, 7), TILES).astype(jnp.int32)


def draw_tile_place(key, part):
    return tile_order(key)


def draw_reader_lists(key, part):
    placed = tile_order(key)
    tile_at = jnp.zeros((TILES,), jnp.int32).at[placed].set(jnp.arange(TILES, dtype=jnp.int32))
    device_count = TILES // TILE_DEV
    readers = jnp.arange(TILES, dtype=jnp.int32)
    own_device = readers // TILE_DEV
    offsets = jnp.concatenate([jnp.arange(-REACH, 0, dtype=jnp.int32), jnp.arange(1, REACH + 1, dtype=jnp.int32)])
    width_cand = 2 * REACH * TILE_DEV
    cand_device = own_device[:, None] + jnp.repeat(offsets, TILE_DEV)[None, :]
    cand_local = jnp.tile(jnp.arange(TILE_DEV, dtype=jnp.int32), 2 * REACH)[None, :]
    usable = (cand_device >= 0) & (cand_device < device_count)
    ranking = jax.random.randint(jax.random.fold_in(key, 11), (TILES, width_cand), 0, 1 << 20) * 128
    ranking = ranking + jnp.arange(width_cand, dtype=jnp.int32)[None, :]
    ranking = jnp.where(usable, ranking, -1)
    unused, picked = lax.top_k(ranking, NEED)
    cand_place = cand_device * TILE_DEV + cand_local
    chosen = jnp.take_along_axis(cand_place, picked, axis=1)
    return tile_at[chosen]


def draw_stale_kv(key, part):
    first_key = jax.random.fold_in(key, 0)
    width = HEADS * HEAD
    base = jnp.clip(jax.random.normal(first_key, (TOKENS, 2 * width), jnp.float32), -6.0, 6.0)
    return base.astype(jnp.bfloat16)


def touch_ends(drawn, stream_key, least, largest):
    shape = drawn.shape
    spot = [jax.random.randint(jax.random.fold_in(stream_key, axis), (), 0, shape[axis]) for axis in range(len(shape))]
    drawn = drawn.at[tuple(spot)].set(least)
    longest = shape.index(max(shape))
    spot[longest] = (spot[longest] + 1) % shape[longest]
    return drawn.at[tuple(spot)].set(largest)


def block_scale(stream_key, dims, cuts, low, high):
    loudness, own = 1.0, jax.random.fold_in(stream_key, 6)
    for dim, blocks in cuts:
        steps = jnp.exp(jax.random.uniform(jax.random.fold_in(own, dim), (blocks,), jnp.float32, low / len(cuts), high / len(cuts)))
        loudness = loudness * jnp.repeat(steps, dims[dim] // blocks).reshape([-1 if axis == dim else 1 for axis in range(len(dims))])
    return loudness


def normal_values(stream_key, extent, scale, reach, cuts=(), kind=jnp.bfloat16):
    drawn = jax.random.normal(stream_key, extent, jnp.float32) * scale
    if len(cuts) > 0:
        drawn = block_scale(stream_key, extent, cuts, -0.22, 0.18) * drawn
    return jnp.clip(drawn, min=-reach, max=reach).astype(kind)


def setup_inputs(seed: int = 0, part: int = 0) -> dict:
    splits = jax.random.split(jax.random.key(seed), 11)
    own_keys = jax.random.split(jax.random.fold_in(splits[10], part), 11)
    tokens = normal_values(own_keys[0], (TOKENS, D), 1.0, 6.0, ((0, 16),))
    mod_shift = normal_values(own_keys[1], (D,), 0.5, 3.0, (), jnp.float32)
    mod_scale = normal_values(own_keys[2], (D,), 0.3, 2.5, (), jnp.float32)
    qkv_weight = normal_values(splits[3], (D, 3 * HW), D ** -0.5, 0.15625, ((0, 16),))
    gain_q = jnp.clip(1.0 + 0.18 * jax.random.normal(splits[4], (HW,), jnp.float32), 0.1, 1.9)
    gain_k = jnp.clip(1.0 + 0.18 * jax.random.normal(splits[5], (HW,), jnp.float32), 0.1, 1.9)
    stale_kv = draw_stale_kv(jax.random.fold_in(jax.random.fold_in(splits[10], part), 71), part)
    tile_place = draw_tile_place(jax.random.fold_in(jax.random.fold_in(splits[10], part), 71), part)
    reader_lists = draw_reader_lists(jax.random.fold_in(jax.random.fold_in(splits[10], part), 71), part)
    window_masks = touch_ends((jax.random.randint(own_keys[9], (TILES, NEED, KB), 0, 3) < 2).astype(jnp.int32), jax.random.fold_in(own_keys[9], 1), 0, 1)
    return dict(tokens=tokens, mod_shift=mod_shift, mod_scale=mod_scale, qkv_weight=qkv_weight, gain_q=gain_q, gain_k=gain_k, stale_kv=stale_kv, tile_place=tile_place, reader_lists=reader_lists, window_masks=window_masks)


def attend(queries, local_keys, local_values, remote, masks):
    tile_dev = queries.shape[0]
    width = HEADS * HEAD
    remote_keys = remote[..., :width].reshape(tile_dev, NEED * TILE, HEADS, HEAD).astype(jnp.float32)
    remote_values = remote[..., width:].reshape(tile_dev, NEED * TILE, HEADS, HEAD).astype(jnp.float32)
    query_f = queries.astype(jnp.float32)
    near = jnp.einsum('rqhe,khe->rhqk', query_f, local_keys.astype(jnp.float32)) * HEAD ** (-0.5)
    far = jnp.einsum('rqhe,rkhe->rhqk', query_f, remote_keys) * HEAD ** (-0.5)
    counted = jnp.repeat(masks.reshape(tile_dev, NEED * KB), KBLK, axis=1) > 0
    counted = counted[:, None, None, :]
    far_kept = jnp.where(counted, far, -jnp.inf)
    top = jnp.maximum(lax.optimization_barrier(jnp.max(near, axis=-1, keepdims=True)), lax.optimization_barrier(jnp.max(far_kept, axis=-1, keepdims=True)))
    near_weights = jnp.exp(near - top)
    far_weights = jnp.where(counted, jnp.exp(far_kept - top), 0.0)
    total = lax.optimization_barrier(jnp.sum(near_weights, axis=-1, keepdims=True)) + lax.optimization_barrier(jnp.sum(far_weights, axis=-1, keepdims=True))
    near_round = near_weights.astype(jnp.bfloat16).astype(jnp.float32)
    far_round = far_weights.astype(jnp.bfloat16).astype(jnp.float32)
    mixed = jnp.einsum('rhqk,khe->rhqe', near_round, local_values.astype(jnp.float32))
    mixed = mixed + jnp.einsum('rhqk,rkhe->rhqe', far_round, remote_values)
    result = (mixed / total).astype(jnp.bfloat16)
    return jnp.transpose(result, (0, 2, 1, 3)).reshape(tile_dev, TILE, width)

def head_norm(values, gain):
    meansq = lax.optimization_barrier(jnp.mean(values * values, axis=-1, keepdims=True))
    return (values * lax.rsqrt(meansq + 1e-06) * gain).astype(jnp.bfloat16)

def reference(tokens, mod_shift, mod_scale, qkv_weight, gain_q, gain_k, stale_kv, tile_place, reader_lists, window_masks):
    width = HEADS * HEAD
    tokens_f = tokens.astype(jnp.float32)
    center = lax.optimization_barrier(jnp.mean(tokens_f, axis=-1, keepdims=True))
    spread = lax.optimization_barrier(jnp.mean((tokens_f - center) ** 2, axis=-1, keepdims=True))
    modulated = ((tokens_f - center) * lax.rsqrt(spread + 1e-06) * (1.0 + mod_scale) + mod_shift).astype(jnp.bfloat16)
    projected = jnp.dot(modulated, qkv_weight, preferred_element_type=jnp.float32)
    query = head_norm(projected[:, :width], gain_q)
    fresh_key = head_norm(projected[:, width:2 * width], gain_k)
    fresh_value = projected[:, 2 * width:].astype(jnp.bfloat16)
    stale_blocks = stale_kv.reshape(TILES, TILE, 2 * width)
    devices = TILES // TILE_DEV

    def one_device(device):
        first = (device * TILE_DEV * TILE).astype(jnp.int32)
        span = TILE_DEV * TILE
        queries = lax.dynamic_slice_in_dim(query, first, span, 0).reshape(TILE_DEV, TILE, HEADS, HEAD)
        local_keys = lax.dynamic_slice_in_dim(fresh_key, first, span, 0).reshape(span, HEADS, HEAD)
        local_values = lax.dynamic_slice_in_dim(fresh_value, first, span, 0).reshape(span, HEADS, HEAD)
        block_first = (device * TILE_DEV).astype(jnp.int32)
        lists = lax.dynamic_slice_in_dim(reader_lists, block_first, TILE_DEV, 0)
        masks = lax.dynamic_slice_in_dim(window_masks, block_first, TILE_DEV, 0)
        places = tile_place[lists]
        remote = stale_blocks[places]
        return attend(queries, local_keys, local_values, remote, masks)
    result = lax.map(one_device, jnp.arange(devices, dtype=jnp.int32))
    return result.reshape(TOKENS, width)
```

```python
import functools

import jax
import jax.numpy as jnp
from jax import lax
from jax.experimental import pallas as pl
from jax.experimental.pallas import tpu as pltpu
from jax.sharding import PartitionSpec as P

HEAD = 128
HEADS = 12
TILE = 384
KBLK = 128
NEED = 2
KB = 3
WIDTH = HEADS * HEAD
HALF = WIDTH // 2
QUART = HALF // 2
GROUPS = 3
COLS = HALF // GROUPS
GHEADS = COLS // HEAD
AXES = ("groups", "seq", "fsdp")

VMEM = pl.BlockSpec(memory_space=pltpu.VMEM)
SMEM = pl.BlockSpec(memory_space=pltpu.SMEM)
ANY = pl.BlockSpec(memory_space=pl.ANY)


def bf16(*shape):
    return jax.ShapeDtypeStruct(shape, jnp.bfloat16)


def f32(*shape):
    return jax.ShapeDtypeStruct(shape, jnp.float32)


def lane(value):
    return pl.multiple_of(value, HEAD)


def parity():
    return lax.rem(lax.axis_index("fsdp"), 2)


def weight_split_kernel(weight, mine, other):
    a, x = parity(), lax.axis_index("groups")
    for out, half in ((mine, a), (other, 1 - a)):
        for part in range(3):
            start = lane(part * WIDTH + half * HALF + x * QUART)
            out[:, part * QUART : (part + 1) * QUART] = weight[:, pl.ds(start, QUART)]


def stale_split_kernel(stale, *outs):
    a = parity()
    for side, half in ((0, a), (1, 1 - a)):
        for g in range(GROUPS):
            out = outs[2 * g + side]
            for part in range(2):
                start = lane(part * WIDTH + half * HALF + g * COLS)
                out[:, part * COLS : (part + 1) * COLS] = stale[:, pl.ds(start, COLS)]


def weight_rows_kernel(*refs):
    pieces, out = refs[:-1], refs[-1]
    z = lax.axis_index("fsdp")
    rows = pieces[0].shape[0]
    for d, piece in enumerate(pieces):
        out[pl.ds(pl.multiple_of((z ^ d) * rows, 32), rows), :] = piece[...]


def modulate_kernel(tokens, shift, scale, out):
    values = tokens[...].astype(jnp.float32)
    center = jnp.mean(values, axis=-1, keepdims=True)
    spread = jnp.mean((values - center) ** 2, axis=-1, keepdims=True)
    out[...] = (
        (values - center) * lax.rsqrt(spread + 1e-06) * (1.0 + scale[...]) + shift[...]
    ).astype(jnp.bfloat16)


def modulate(tokens, shift, scale):
    rows = KBLK
    return pl.pallas_call(
        modulate_kernel,
        grid=(TILE // rows,),
        out_shape=bf16(TILE, WIDTH),
        in_specs=[
            pl.BlockSpec((rows, WIDTH), lambda i: (i, 0)),
            pl.BlockSpec((1, WIDTH), lambda i: (0, 0)),
            pl.BlockSpec((1, WIDTH), lambda i: (0, 0)),
        ],
        out_specs=pl.BlockSpec((rows, WIDTH), lambda i: (i, 0)),
        cost_estimate=pl.CostEstimate(
            flops=10 * TILE * WIDTH, bytes_accessed=4 * TILE * WIDTH, transcendentals=0
        ),
        name="modulate",
    )(tokens, shift, scale)


def project_kernel(places, mod0, mod1, *refs):
    count = len(places)
    weights, (q, k, v, ssq, held, sems) = refs[:count], refs[count:]
    copies = []
    for i, place in enumerate(places):
        for part, src_row, src, row, col, rows, cols in place():
            copies.append(
                pltpu.make_async_copy(
                    weights[i].at[pl.ds(src_row, rows), pl.ds(src, cols)],
                    held.at[pl.ds(row, rows), pl.ds(col, cols)],
                    sems.at[len(copies)],
                )
            )
    for copy in copies:
        copy.start()
    for copy in copies:
        copy.wait()
    step = 2 * HEAD
    lanes = lax.broadcasted_iota(jnp.int32, (TILE, HEAD), 1)
    stats = jnp.zeros((TILE, HEAD), jnp.float32)
    for part, out in enumerate((q, k, v)):

        def chunk(i, sums, part=part, out=out):
            col = lane(part * HALF + i * step)
            panel = held[:, pl.ds(col, step)]
            fresh = []
            for unit, mod in enumerate((mod0, mod1)):
                got = jnp.dot(mod[...], panel, preferred_element_type=jnp.float32)
                out[unit, :, pl.ds(lane(i * step), step)] = got.astype(out.dtype)
                if part < 2:
                    fresh.append(sums[unit] + jnp.sum(got * got, axis=-1, keepdims=True))
            return tuple(fresh) if part < 2 else sums

        zero = jnp.zeros((TILE, 1), jnp.float32)
        sums = lax.fori_loop(0, HALF // step, chunk, (zero, zero))
        if part < 2:
            for unit in range(2):
                stats = jnp.where(lanes == 2 * unit + part, sums[unit], stats)
    ssq[...] = stats


def project(mods, weights, places, ncopies):
    return pl.pallas_call(
        functools.partial(project_kernel, places),
        out_shape=(
            f32(2, TILE, HALF),
            f32(2, TILE, HALF),
            bf16(2, TILE, HALF),
            f32(TILE, HEAD),
        ),
        in_specs=[VMEM, VMEM] + [ANY] * len(weights),
        out_specs=(VMEM,) * 4,
        scratch_shapes=[
            pltpu.VMEM((WIDTH, 3 * HALF), jnp.bfloat16),
            pltpu.SemaphoreType.DMA((ncopies,)),
        ],
        cost_estimate=pl.CostEstimate(
            flops=2 * 2 * TILE * WIDTH * 3 * HALF,
            bytes_accessed=2 * WIDTH * 3 * HALF,
            transcendentals=0,
        ),
        name="project",
    )(*mods, *weights)


def attend_kernel(
    group, relay, place, lists, masks, pinfo, q, k, v, ssq, rssq, gain_q, gain_k, *refs
):
    cands, (own_out, part_out, held, sems) = refs[:6], refs[6:]
    step = pl.program_id(0)
    unit, head = step // GHEADS, lax.rem(step, GHEADS)
    seq, z = lax.axis_index("seq"), lax.axis_index("fsdp")
    a = lax.rem(z, 2)
    pairs = lax.axis_size("fsdp") // 2
    pair_in, pair = z // 2, seq * pairs + z // 2

    @pl.when(step == 0)
    def _():
        for u in range(2):
            for n in range(NEED):
                tile = lists[0, n] if u == 0 else pinfo[n]
                slot = place[tile] - 2 * pair + 2
                offset = slot // 2 - 1
                other = (lax.rem(slot, 2) != a).astype(jnp.int32)
                if relay:
                    inside = jnp.where(pair_in == 0, offset == 1, offset == -1)
                    kind = jnp.where(inside, 1, 2)
                else:
                    kind = jnp.where(offset == 1, 1, 2)
                cand = 2 * jnp.where(offset == 0, 0, kind) + other
                for i in range(6):

                    @pl.when(cand == i)
                    def _(i=i, e=2 * u + n):
                        pltpu.make_async_copy(cands[i], held.at[e], sems.at[e]).start()

    @pl.when(head == 0)
    def _():
        for n in range(NEED):
            e = 2 * unit + n
            pltpu.make_async_copy(cands[0], held.at[e], sems.at[e]).wait()

    def total(item):
        mine = jnp.where(unit == 0, ssq[:, item : item + 1], ssq[:, 2 + item : 3 + item])
        far = jnp.where(unit == 0, rssq[:, 2 + item : 3 + item], rssq[:, item : item + 1])
        return lax.rsqrt((mine + far) * (1.0 / WIDTH) + 1e-06)

    cols = pl.ds(lane(a * HALF + group * COLS + head * HEAD), HEAD)
    query = (q[0] * total(0) * gain_q[:, cols]).astype(jnp.bfloat16)
    key = (k[0] * total(1) * gain_k[:, cols]).astype(jnp.bfloat16)

    def score(keys):
        return lax.dot_general(
            query, keys, (((1,), (1,)), ((), ())), preferred_element_type=jnp.float32
        )

    def masked(n):
        block = lax.broadcasted_iota(jnp.int32, (1, TILE), 1) // KBLK
        bias = jnp.zeros((1, TILE), jnp.float32)
        for b in range(KB):
            flag = jnp.where(
                unit == 0, masks[0, n, b], pinfo[NEED + n * KB + b]
            )
            gone = jnp.where(flag > 0, 0.0, -jnp.inf).astype(jnp.float32)
            bias = jnp.where(block == b, gone, bias)
        return bias

    scores = [score(key)]
    values = [v[0]]
    for n in range(NEED):
        e = 2 * unit + n
        far_key = held[e, :, pl.ds(lane(head * HEAD), HEAD)]
        scores.append(score(far_key) + masked(n))
        values.append(held[e, :, pl.ds(lane(COLS + head * HEAD), HEAD)])
    top = functools.reduce(
        jnp.maximum, [jnp.max(s, axis=-1, keepdims=True) for s in scores]
    )
    weights = [jnp.exp((s - top) * HEAD ** (-0.5)) for s in scores]
    sums = sum(jnp.sum(w, axis=-1, keepdims=True) for w in weights)
    mixed = sum(
        jnp.dot(w.astype(jnp.bfloat16), x, preferred_element_type=jnp.float32)
        for w, x in zip(weights, values)
    )
    result = (mixed / sums).astype(jnp.bfloat16)

    @pl.when(unit == 0)
    def _():
        own_out[...] = result

    @pl.when(unit == 1)
    def _():
        part_out[...] = result


def attend(group, relay, place, lists, masks, pinfo, q, k, v, ssq, rssq, gains, cands):
    head = lambda i: (i // GHEADS, 0, group * GHEADS + lax.rem(i, GHEADS))
    whole = lambda i: (0, 0)
    return pl.pallas_call(
        functools.partial(attend_kernel, group, relay),
        grid=(2 * GHEADS,),
        out_shape=(bf16(TILE, COLS), bf16(TILE, COLS)),
        in_specs=[SMEM] * 4
        + [pl.BlockSpec((1, TILE, HEAD), head)] * 3
        + [pl.BlockSpec((TILE, HEAD), whole)] * 2
        + [pl.BlockSpec((1, WIDTH), whole)] * 2
        + [ANY] * 6,
        out_specs=(
            pl.BlockSpec((TILE, HEAD), lambda i: (0, jnp.minimum(i, GHEADS - 1))),
            pl.BlockSpec((TILE, HEAD), lambda i: (0, jnp.maximum(i - GHEADS, 0))),
        ),
        scratch_shapes=[
            pltpu.VMEM((2 * NEED, TILE, 2 * COLS), jnp.bfloat16),
            pltpu.SemaphoreType.DMA((2 * NEED,)),
        ],
        cost_estimate=pl.CostEstimate(
            flops=2 * GHEADS * 4 * TILE * 3 * TILE * HEAD,
            bytes_accessed=12 * TILE * COLS,
            transcendentals=2 * GHEADS * TILE * 3 * TILE,
        ),
        name=f"attend{group}",
    )(place, lists, masks, pinfo, q, k, v, ssq, rssq, *gains, *cands)


def join_kernel(*refs):
    pieces, out = refs[:-1], refs[-1]
    a = parity()
    for i, piece in enumerate(pieces):
        side, g = divmod(i, GROUPS)
        half = a if side == 0 else 1 - a
        out[:, pl.ds(lane(half * HALF + g * COLS), COLS)] = piece[...]


def on_device(
    tokens,
    mod_shift,
    mod_scale,
    qkv_weight,
    gain_q,
    gain_k,
    stale_kv,
    tile_place,
    reader_lists,
    window_masks,
):
    jobs, seqs, lines = (lax.axis_size(name) for name in AXES)
    relay = lines == 4

    def send(block, target):
        route = []
        for g in range(jobs):
            for s in range(seqs):
                for z in range(lines):
                    to = target(g, s, z)
                    if to is not None:
                        source = (g * seqs + s) * lines + z
                        route.append((source, (to[0] * seqs + to[1]) * lines + to[2]))
        return lax.ppermute(block, AXES, route)

    def across(distance):
        return lambda g, s, z: (g, s, z ^ distance)

    def along(shift, flip):
        def target(g, s, z):
            r = s * lines + z + shift
            if not 0 <= r < seqs * lines:
                return None
            r ^= flip
            return (g, r // lines, r % lines)

        return target

    def wrap(g, s, z):
        t = s + 1 if z < 2 else s - 1
        return (g, t, z) if 0 <= t < seqs else None

    info = jnp.concatenate([reader_lists.reshape(-1), window_masks.reshape(-1)])
    near_tokens = send(tokens, across(1))
    near_info = send(info, across(1))

    split_weights = relay and seqs == 4 and jobs == 2
    rows = qkv_weight.shape[0]
    if split_weights:
        mine, other = pl.pallas_call(
            weight_split_kernel,
            out_shape=(bf16(rows, 3 * QUART),) * 2,
            in_specs=[VMEM],
            out_specs=(VMEM,) * 2,
            name="weight_split",
        )(qkv_weight)
        line = [mine] + [send(other if d % 2 else mine, across(d)) for d in (1, 2, 3)]

    pieces = pl.pallas_call(
        stale_split_kernel,
        out_shape=(bf16(TILE, 2 * COLS),) * (2 * GROUPS),
        in_specs=[VMEM],
        out_specs=(VMEM,) * (2 * GROUPS),
        name="stale_split",
    )(stale_kv)

    cands = []
    for g in range(GROUPS):
        mine_kv, other_kv = pieces[2 * g : 2 * g + 2]
        beside = send(other_kv, across(1))
        if relay:
            far = [send(mine_kv, across(2)), send(other_kv, across(3))]
            far += [send(block, wrap) for block in far]
        else:
            far = [
                send(block, along(shift, flip))
                for shift in (-2, 2)
                for block, flip in ((mine_kv, 0), (other_kv, 1))
            ]
        cands.append([mine_kv, beside] + far)

    shift, scale = mod_shift.reshape(1, -1), mod_scale.reshape(1, -1)
    mods = [modulate(block, shift, scale) for block in (tokens, near_tokens)]

    if split_weights:
        own = pl.pallas_call(
            weight_rows_kernel,
            out_shape=bf16(lines * rows, 3 * QUART),
            in_specs=[VMEM] * 4,
            out_specs=VMEM,
            name="weight_rows",
        )(*line)
        held = [own]
        for flip_g, flip_s in ((0, 2), (1, 0), (1, 2)):
            held.append(send(own, lambda g, s, z: (g ^ flip_g, s ^ flip_s, z)))
        weights, places = [], []
        for turn in (0, 1):
            for (flip_g, flip_s), block in zip(((0, 0), (0, 2), (1, 0), (1, 2)), held):
                if turn:
                    block = send(block, lambda g, s, z: (g, s ^ 1, z))

                def place(flip_g=flip_g, flip_s=flip_s ^ turn):
                    x = lax.axis_index("groups") ^ flip_g
                    row = pl.multiple_of((lax.axis_index("seq") ^ flip_s) * TILE, TILE)
                    return [
                        (p, 0, p * QUART, row, lane(p * HALF + x * QUART), TILE, QUART)
                        for p in range(3)
                    ]

                weights.append(block)
                places.append(place)
        ncopies = 24
    else:
        panel = lax.all_gather(qkv_weight, "fsdp", axis=0, tiled=True)
        weights = [lax.all_gather(panel, "seq", axis=0, tiled=True)]

        def place():
            a = parity()
            return [
                (p, 0, lane(p * WIDTH + a * HALF), 0, p * HALF, WIDTH, HALF)
                for p in range(3)
            ]

        places, ncopies = [place], 3
    q, k, v, ssq = project(mods, weights, places, ncopies)
    near_ssq = send(ssq, across(1))

    gains = (gain_q.reshape(1, -1), gain_k.reshape(1, -1))
    own_parts, near_parts = [], []
    for g in range(GROUPS):
        own, part = attend(
            g, relay, tile_place, reader_lists, window_masks, near_info,
            q, k, v, ssq, near_ssq, gains, cands[g],
        )
        own_parts.append(own)
        near_parts.append(send(part, across(1)))
    return pl.pallas_call(
        join_kernel,
        out_shape=bf16(TILE, WIDTH),
        in_specs=[VMEM] * (2 * GROUPS),
        out_specs=VMEM,
        name="join",
    )(*own_parts, *near_parts)


def solution(mesh):
    rows = P(("groups", "seq", "fsdp"), None)
    placed = (
        rows,
        P("groups"),
        P("groups"),
        P(("seq", "fsdp"), None),
        P(),
        P(),
        rows,
        P("groups"),
        rows,
        P(("groups", "seq", "fsdp"), None, None),
    )
    return jax.shard_map(
        on_device, mesh=mesh, in_specs=placed, out_specs=rows, check_vma=False
    )
```

```python
import functools
import math

import jax
import jax.numpy as jnp
from jax import lax
from jax.experimental import pallas as pl
from jax.experimental.pallas import tpu as pltpu
from jax.sharding import PartitionSpec as P


HEAD = 128
HEADS = 12
TILE = 384
KBLK = 128
NEED = 2
KB = 3
WIDTH = HEADS * HEAD
HALF = WIDTH // 2
QUART = HALF // 2
SPLIT = (2, 2, 2)
GROUPS = len(SPLIT)
FIRST = tuple(sum(SPLIT[:g]) for g in range(GROUPS))
ROWS = 192
AXES = ("groups", "seq", "fsdp")

VMEM = pl.BlockSpec(memory_space=pltpu.VMEM)
SMEM = pl.BlockSpec(memory_space=pltpu.SMEM)
HBM = pl.BlockSpec(memory_space=pltpu.HBM)
PARAMS = pltpu.CompilerParams(vmem_limit_bytes=67_000_000)
SCALE = HEAD ** (-0.5) / math.log(2.0)


def bf16(*shape):
    return jax.ShapeDtypeStruct(shape, jnp.bfloat16)


def f32(*shape):
    return jax.ShapeDtypeStruct(shape, jnp.float32)


def lane(value):
    return pl.multiple_of(value, HEAD)


def parity():
    return lax.rem(lax.axis_index("fsdp"), 2)


def weight_split_kernel(weight, mine, other):
    a, x = parity(), lax.axis_index("groups")
    for out, half in ((mine, a), (other, 1 - a)):
        for part in range(3):
            start = lane(part * WIDTH + half * HALF + x * QUART)
            out[:, part * QUART : (part + 1) * QUART] = weight[:, pl.ds(start, QUART)]


def stale_split_kernel(lists, masks, stale, info, *outs):
    for n in range(NEED):
        info[n] = lists[0, n]
        for b in range(KB):
            info[NEED + n * KB + b] = masks[0, n, b]
    a = parity()
    for side, half in ((0, a), (1, 1 - a)):
        for g in range(GROUPS):
            out, cols = outs[2 * g + side], SPLIT[g] * HEAD
            for part in range(2):
                start = lane(part * WIDTH + half * HALF + FIRST[g] * HEAD)
                out[:, part * cols : (part + 1) * cols] = stale[:, pl.ds(start, cols)]


def weight_rows_kernel(*refs):
    pieces, out = refs[:-1], refs[-1]
    z = lax.axis_index("fsdp")
    rows = pieces[0].shape[0]
    for d, piece in enumerate(pieces):
        out[pl.ds(pl.multiple_of((z ^ d) * rows, 32), rows), :] = piece[...]


def modulate_kernel(tokens, shift, scale, out):
    values = tokens[...].astype(jnp.float32)
    center = jnp.mean(values, axis=-1, keepdims=True)
    spread = jnp.mean((values - center) ** 2, axis=-1, keepdims=True)
    out[...] = (
        (values - center) * lax.rsqrt(spread + 1e-06) * (1.0 + scale[...][None]) + shift[...][None]
    ).astype(jnp.bfloat16)


def modulate(tokens, shift, scale):
    rows = KBLK
    return pl.pallas_call(
        modulate_kernel,
        grid=(TILE // rows,),
        out_shape=bf16(TILE, WIDTH),
        in_specs=[
            pl.BlockSpec((rows, WIDTH), lambda i: (i, 0)),
            pl.BlockSpec((WIDTH,), lambda i: (0,)),
            pl.BlockSpec((WIDTH,), lambda i: (0,)),
        ],
        out_specs=pl.BlockSpec((rows, WIDTH), lambda i: (i, 0)),
        cost_estimate=pl.CostEstimate(
            flops=10 * TILE * WIDTH, bytes_accessed=4 * TILE * WIDTH, transcendentals=0
        ),
        compiler_params=PARAMS,
        name="modulate",
    )(tokens, shift, scale)


def project_kernel(places, parts, mod0, mod1, *refs):
    count = len(places)
    weights, refs = refs[:count], refs[count:]
    out, (held, sems) = refs[0], refs[-2:]
    index = pl.program_id(0)
    copies = [[] for _ in parts]
    for i, place in enumerate(places):
        for p, src, row, col, rows, cols in place():
            if p in parts:
                n = parts.index(p)
                copies[n].append(
                    pltpu.make_async_copy(
                        weights[i].at[:, pl.ds(src, cols)],
                        held.at[n, pl.ds(row, rows), pl.ds(col, cols)],
                        sems.at[n, i],
                    )
                )

    @pl.when(index == 0)
    def _():
        for group in copies:
            for copy in group:
                copy.start()

    for n, group in enumerate(copies):

        @pl.when(index == n)
        def _(group=group):
            for copy in group:
                copy.wait()

    step = 2 * HEAD
    sums = [jnp.zeros((TILE, HEAD), jnp.float32)] * 2
    for i in range(HALF // step):
        cols = slice(i * step, (i + 1) * step)
        panel = held[index, :, cols]
        for unit, mod in enumerate((mod0, mod1)):
            got = jnp.dot(mod[...], panel, preferred_element_type=jnp.float32)
            out[0, unit, :, cols] = got.astype(out.dtype)
            square = got * got
            sums[unit] = sums[unit] + square[:, :HEAD] + square[:, HEAD:]
    if len(parts) > 1:
        ssq, stats = refs[1:3]
        lanes = lax.broadcasted_iota(jnp.int32, (TILE, HEAD), 1)
        now = jnp.where(index == 0, 0.0, stats[...])
        for unit in range(2):
            total = jnp.sum(sums[unit], axis=-1, keepdims=True)
            now = jnp.where(lanes == 2 * unit + index, total, now)
        stats[...] = now

        @pl.when(index == len(parts) - 1)
        def _():
            ssq[...] = stats[...].T[:8]


def project(mods, weights, places, parts):
    whole = lambda i: (0, 0)
    count = len(parts)
    kind = f32 if count > 1 else bf16
    norms = count > 1
    return pl.pallas_call(
        functools.partial(project_kernel, places, parts),
        grid=(count,),
        out_shape=(kind(count, 2, TILE, HALF),) + (f32(8, TILE),) * norms,
        in_specs=[pl.BlockSpec((TILE, WIDTH), whole)] * 2 + [HBM] * len(weights),
        out_specs=(pl.BlockSpec((1, 2, TILE, HALF), lambda i: (i, 0, 0, 0)),)
        + (pl.BlockSpec((8, TILE), whole),) * norms,
        scratch_shapes=[pltpu.VMEM((TILE, HEAD), jnp.float32)] * norms
        + [
            pltpu.VMEM((count, WIDTH, HALF), jnp.bfloat16),
            pltpu.SemaphoreType.DMA((count, len(weights))),
        ],
        cost_estimate=pl.CostEstimate(
            flops=2 * 2 * TILE * WIDTH * count * HALF,
            bytes_accessed=2 * WIDTH * count * HALF,
            transcendentals=0,
        ),
        compiler_params=PARAMS,
    )(*mods, *weights)


def attend_kernel(
    group, units, relay, place, lists, masks, pinfo, q, k, v, ssq, rssq, gain_q, gain_k, *refs
):
    heads, cols = SPLIT[group], SPLIT[group] * HEAD
    cands, refs = refs[:6], refs[6:]
    outs, (keys, values, factors, sems) = refs[: len(units)], refs[len(units) :]
    turn = pl.program_id(0)
    unit = jnp.where(turn == 0, units[0], units[-1])
    seq, z = lax.axis_index("seq"), lax.axis_index("fsdp")
    a = lax.rem(z, 2)
    pairs = lax.axis_size("fsdp") // 2
    pair_in, pair = z // 2, seq * pairs + z // 2

    def fetch(i, t, n):
        return [
            pltpu.make_async_copy(
                cands[i].at[:, pl.ds(kind * cols, cols)],
                held.at[t, pl.ds((n + 1) * TILE, TILE)],
                sems.at[t, n, kind],
            )
            for kind, held in enumerate((keys, values))
        ]

    @pl.when(turn == 0)
    def _():
        for t, u in enumerate(units):
            for n in range(NEED):
                tile = lists[0, n] if u == 0 else pinfo[n]
                slot = place[tile] - 2 * pair + 2
                offset = slot // 2 - 1
                other = (lax.rem(slot, 2) != a).astype(jnp.int32)
                if relay:
                    inside = jnp.where(pair_in == 0, offset == 1, offset == -1)
                    kind = jnp.where(inside, 1, 2)
                else:
                    kind = jnp.where(offset == 1, 1, 2)
                cand = 2 * jnp.where(offset == 0, 0, kind) + other
                for i in range(6):

                    @pl.when(cand == i)
                    def _(i=i, t=t, n=n):
                        for copy in fetch(i, t, n):
                            copy.start()

        for t, u in enumerate(units):
            rows = [
                ssq[2 * u + i : 2 * u + i + 1] + rssq[2 - 2 * u + i : 3 - 2 * u + i]
                for i in range(2)
            ]
            rows = jnp.concatenate(rows + [jnp.ones((6, TILE), jnp.float32)])
            scale = lax.rsqrt(rows * (1.0 / WIDTH) + 1e-06).T
            for i in range(2):
                factors[t, i] = jnp.broadcast_to(scale[:, i : i + 1], (TILE, HEAD))

    def normed(part, item, gains, h):
        gain = gains[pl.ds(lane(a * HALF + (FIRST[group] + h) * HEAD), HEAD)]
        value = part[0, 0, :, h * HEAD : (h + 1) * HEAD]
        return (value * factors[turn, item] * gain[None]).astype(jnp.bfloat16)

    def score(queries, keys):
        return lax.dot_general(
            queries, keys, (((1,), (1,)), ((), ())), preferred_element_type=jnp.float32
        )

    gone = []
    for n in range(NEED):
        for b in range(KB):
            flag = jnp.where(unit == 0, masks[0, n, b], pinfo[NEED + n * KB + b])
            gone.append(jnp.where(flag > 0, 0.0, -jnp.inf).astype(jnp.float32))

    keys[turn, :TILE] = jnp.concatenate(
        [normed(k, 1, gain_k, h) for h in range(heads)], axis=1
    )
    values[turn, :TILE] = v[0, 0]
    queries = [normed(q, 0, gain_q, h) for h in range(heads)]
    for n in range(NEED):
        for copy in fetch(0, turn, n):
            copy.wait()
    blocks = (NEED + 1) * KB

    def scores(h, r):
        some = queries[h][r * ROWS : (r + 1) * ROWS]
        whole = score(some, keys[turn, :, h * HEAD : (h + 1) * HEAD])
        parts = [whole[:, b * KBLK : (b + 1) * KBLK] for b in range(blocks)]
        return [p + gone[b - KB] if b >= KB else p for b, p in enumerate(parts)]

    def finish(h, parts):
        top = jnp.max(functools.reduce(jnp.maximum, parts), axis=-1, keepdims=True)
        parts = [jnp.exp2((p - top) * SCALE) for p in parts]
        sums = jnp.sum(functools.reduce(jnp.add, parts), axis=-1, keepdims=True)
        weights = jnp.concatenate([p.astype(jnp.bfloat16) for p in parts], axis=1)
        value = values[turn, :, h * HEAD : (h + 1) * HEAD]
        mixed = jnp.dot(weights, value, preferred_element_type=jnp.float32)
        return (mixed / sums).astype(jnp.bfloat16)

    tasks = [(h, r) for h in range(heads) for r in range(TILE // ROWS)]
    results, ahead = [], scores(*tasks[0])
    for i, (h, r) in enumerate(tasks):
        now = ahead
        if i + 1 < len(tasks):
            ahead = scores(*tasks[i + 1])
        results.append((h, r, finish(h, now)))

    for t, out in enumerate(outs):

        @pl.when(turn == t)
        def _(out=out):
            for h, r, result in results:
                out[r * ROWS : (r + 1) * ROWS, h * HEAD : (h + 1) * HEAD] = result


def attend(group, units, relay, place, lists, masks, pinfo, qk, v, ssq, rssq, gains, cands):
    heads, cols, count = SPLIT[group], SPLIT[group] * HEAD, len(units)

    def head(i):
        return (jnp.where(i == 0, units[0], units[-1]), 0, FIRST[group] // heads)

    whole = lambda i: (0, 0)
    blocks = [
        pl.BlockSpec((1, 1, TILE, cols), lambda i, p=p: (p,) + head(i)) for p in (0, 1, 0)
    ]
    return pl.pallas_call(
        functools.partial(attend_kernel, group, units, relay),
        grid=(count,),
        out_shape=(bf16(TILE, cols),) * count,
        in_specs=[SMEM] * 4
        + blocks
        + [pl.BlockSpec((8, TILE), whole)] * 2
        + [pl.BlockSpec((WIDTH,), lambda i: (0,))] * 2
        + [HBM] * 6,
        out_specs=(pl.BlockSpec((TILE, cols), whole),) * count,
        scratch_shapes=[
            pltpu.VMEM((count, (NEED + 1) * TILE, cols), jnp.bfloat16),
            pltpu.VMEM((count, (NEED + 1) * TILE, cols), jnp.bfloat16),
            pltpu.VMEM((count, 2, TILE, HEAD), jnp.float32),
            pltpu.SemaphoreType.DMA((count, NEED, 2)),
        ],
        cost_estimate=pl.CostEstimate(
            flops=count * heads * 4 * TILE * 3 * TILE * HEAD,
            bytes_accessed=6 * count * TILE * cols,
            transcendentals=count * heads * TILE * 3 * TILE,
        ),
        compiler_params=PARAMS,
    )(place, lists, masks, pinfo, qk, qk, v, ssq, rssq, *gains, *cands)


def join_kernel(*refs):
    pieces, out = refs[:-1], refs[-1]
    a = parity()
    for i, piece in enumerate(pieces):
        side, g = divmod(i, GROUPS)
        half = a if side == 0 else 1 - a
        start = lane(half * HALF + FIRST[g] * HEAD)
        out[:, pl.ds(start, SPLIT[g] * HEAD)] = piece[...]


def on_device(
    tokens,
    mod_shift,
    mod_scale,
    qkv_weight,
    gain_q,
    gain_k,
    stale_kv,
    tile_place,
    reader_lists,
    window_masks,
):
    jobs, seqs, lines = (lax.axis_size(name) for name in AXES)
    relay = lines == 4

    def send(block, target):
        route = []
        for g in range(jobs):
            for s in range(seqs):
                for z in range(lines):
                    to = target(g, s, z)
                    if to is not None:
                        source = (g * seqs + s) * lines + z
                        route.append((source, (to[0] * seqs + to[1]) * lines + to[2]))
        return lax.ppermute(block, AXES, route)

    def across(distance):
        return lambda g, s, z: (g, s, z ^ distance)

    def along(shift, flip):
        def target(g, s, z):
            r = s * lines + z + shift
            if not 0 <= r < seqs * lines:
                return None
            r ^= flip
            return (g, r // lines, r % lines)

        return target

    def wrap(g, s, z):
        t = s + 1 if z < 2 else s - 1
        return (g, t, z) if 0 <= t < seqs else None

    near_tokens = send(tokens, across(1))

    split_weights = relay and seqs == 4 and jobs == 2
    rows = qkv_weight.shape[0]
    if split_weights:
        mine, other = pl.pallas_call(
            weight_split_kernel,
            out_shape=(bf16(rows, 3 * QUART),) * 2,
            in_specs=[VMEM],
            out_specs=(VMEM,) * 2,
            compiler_params=PARAMS,
            name="weight_split",
        )(qkv_weight)
        line = [mine] + [send(other if d % 2 else mine, across(d)) for d in (1, 2, 3)]

    info, *pieces = pl.pallas_call(
        stale_split_kernel,
        out_shape=(jax.ShapeDtypeStruct((NEED + NEED * KB,), jnp.int32),)
        + tuple(bf16(TILE, 2 * n * HEAD) for n in SPLIT for _ in range(2)),
        in_specs=[SMEM, SMEM, VMEM],
        out_specs=(SMEM,) + (VMEM,) * (2 * GROUPS),
        compiler_params=PARAMS,
        name="stale_split",
    )(reader_lists, window_masks, stale_kv)
    near_info = send(info, across(1))

    cands = []
    for g in range(GROUPS):
        mine_kv, other_kv = pieces[2 * g : 2 * g + 2]
        beside = send(other_kv, across(1))
        if relay:
            far = [send(mine_kv, across(2)), send(other_kv, across(3))]
            far += [send(block, wrap) for block in far]
        else:
            far = [
                send(block, along(shift, flip))
                for shift in (-2, 2)
                for block, flip in ((mine_kv, 0), (other_kv, 1))
            ]
        cands.append([mine_kv, beside] + far)

    mods = []
    for block in (tokens, near_tokens):
        mods.append(modulate(block, mod_shift, mod_scale))

    if split_weights:
        own = pl.pallas_call(
            weight_rows_kernel,
            out_shape=bf16(lines * rows, 3 * QUART),
            in_specs=[VMEM] * 4,
            out_specs=VMEM,
            compiler_params=PARAMS,
            name="weight_rows",
        )(*line)
        held = [own]
        for flip_g, flip_s in ((0, 2), (1, 0), (1, 2)):
            held.append(send(own, lambda g, s, z: (g ^ flip_g, s ^ flip_s, z)))
        weights, places = [], []
        for turn in (0, 1):
            flips = ((0, 0), (0, 2), (1, 0), (1, 2))
            for (flip_g, flip_s), block in zip(flips, held):
                if turn:
                    block = send(block, lambda g, s, z: (g, s ^ 1, z))

                def place(flip_g=flip_g, flip_s=flip_s ^ turn):
                    x = lax.axis_index("groups") ^ flip_g
                    row = pl.multiple_of((lax.axis_index("seq") ^ flip_s) * TILE, TILE)
                    return [
                        (p, p * QUART, row, lane(x * QUART), TILE, QUART)
                        for p in range(3)
                    ]

                weights.append(block)
                places.append(place)
    else:
        panel = lax.all_gather(qkv_weight, "fsdp", axis=0, tiled=True)
        weights = [lax.all_gather(panel, "seq", axis=0, tiled=True)]

        def place():
            a = parity()
            return [
                (p, lane(p * WIDTH + a * HALF), 0, 0, WIDTH, HALF)
                for p in range(3)
            ]

        places = [place]
    qk, ssq = project(mods, weights, places, (0, 1))
    (v,) = project(mods, weights, places, (2,))
    near_ssq = send(ssq, across(1))

    gains = (gain_q, gain_k)
    own_parts, near_parts = [], []
    for g in range(GROUPS):
        turns = ((1,), (0,)) if g == GROUPS - 1 else ((1, 0),)
        done = []
        for units in turns:
            done += attend(
                g, units, relay, tile_place, reader_lists, window_masks, near_info,
                qk, v, ssq, near_ssq, gains, cands[g],
            )
        part, own = done
        own_parts.append(own)
        near_parts.append(send(part, across(1)))
    return pl.pallas_call(
        join_kernel,
        out_shape=bf16(TILE, WIDTH),
        in_specs=[VMEM] * (2 * GROUPS),
        out_specs=VMEM,
        compiler_params=PARAMS,
        name="join",
    )(*own_parts, *near_parts)


def solution(mesh):
    rows = P(("groups", "seq", "fsdp"), None)
    placed = (
        rows,
        P("groups"),
        P("groups"),
        P(("seq", "fsdp"), None),
        P(),
        P(),
        rows,
        P("groups"),
        rows,
        P(("groups", "seq", "fsdp"), None, None),
    )
    return jax.shard_map(
        on_device, mesh=mesh, in_specs=placed, out_specs=rows, check_vma=False
    )
```
